32 devices in a mesh: row: 8 (over y, x, core), col: 4 (over z).
Axes of the slice: x: 2, y: 2, z: 4, core: 2. Of those that a mesh axis runs over, the one named last changes fastest.
Arguments:
- key_rows: float32 [128, 20480], P('col', 'row'), may hold values from -0.0390625 to 0.0390625
- targets: float32 [128, 7168], P(None, 'col'), may hold values from -24 to 24
- weight: float32 [20480, 7168], P('row', 'col'), may hold values from -6 to 6
- covariance: float32 [20480, 20480], P('row', 'col'), may hold values from -3 to 24, as said below
Outputs:
- increment: float32 [20480, 7168], P('row', 'col')
The draws below stay inside these ranges and needn't reach their ends.
Inputs may be any that keep to these rules, and one draw needn't show every extreme that they name: covariance is symmetric and positive definite.
All inputs are finite; a program needn't handle non-finite values.
Results may differ from the reference program's by a relative error of at most 0.0003.
Values sent between devices are 32-bit elements; how exact they have to be, the bound alone decides.
No kernel may reach another device: no remote copies, remote signals or barrier semaphores. Data moves between devices by JAX's collectives and lax.ppermute only.
A program may use at most 192 MiB of HBM per device.

```python
import jax
import jax.numpy as jnp
from jax import lax

D_IN = 20480
D_OUT = 7168
R = 128


def draw_covariance(key, part):
    key_noise = jax.random.fold_in(key, 11)
    key_diag = jax.random.fold_in(key, 12)
    noise_draw = jax.random.normal(key_noise, (D_IN, D_IN), jnp.float32)
    offdiag = 0.4 * (noise_draw + noise_draw.T) / jnp.sqrt(2.0 * D_IN)
    offdiag = offdiag * (1.0 - jnp.eye(D_IN, dtype=jnp.float32))
    diagonal = jax.random.uniform(key_diag, (D_IN,), jnp.float32, 1.0, 2.6)
    matrix = offdiag + jnp.diag(diagonal)
    return matrix


def steps_of(stream_key, extent, cuts, low, largest):
    def one(position, parts):
        heights = jax.random.uniform(jax.random.fold_in(jax.random.fold_in(stream_key, 6), position), (parts,), jnp.float32, low / len(cuts), largest / len(cuts))
        return jnp.repeat(jnp.exp(heights), extent[position] // parts).reshape((-1,) + (1,) * (len(extent) - position - 1))

    level = one(*cuts[0])
    for cut in cuts[1:]:
        level = level * one(*cut)
    return level


def centred(key, shape, scale, bound, shards=(), kind=jnp.bfloat16):
    level = steps_of(key, shape, shards, -0.22, 0.18) if shards else 1.0
    result = jax.random.normal(key, shape, jnp.float32) * scale * level
    return jnp.minimum(jnp.maximum(result, -bound), bound).astype(kind)


def setup_inputs(seed: int = 0) -> dict:
    streams_of = jax.random.split(jax.random.key(seed), 5)
    key_rows = centred(streams_of[0], (R, D_IN), D_IN ** -0.5, 0.0390625, ((0, 4), (1, 8)), jnp.float32)
    targets = centred(streams_of[1], (R, D_OUT), 4.0, 24.0, ((1, 4),), jnp.float32)
    weight = centred(streams_of[2], (D_IN, D_OUT), 1.0, 6.0, ((0, 8), (1, 4)), jnp.float32)
    covariance = draw_covariance(jax.random.fold_in(streams_of[4], 71), 0)
    return dict(key_rows=key_rows, targets=targets, weight=weight, covariance=covariance)


def precise(left, right):
    return jnp.dot(left.astype(jnp.float32), right.astype(jnp.float32), precision=lax.Precision.HIGHEST, preferred_element_type=jnp.float32)

def reference(key_rows, targets, weight, covariance):
    residual = targets - precise(key_rows, weight)
    basis_panel = key_rows.T
    gram_keys = precise(key_rows, basis_panel)
    image_one = precise(covariance, basis_panel) + precise(basis_panel, gram_keys)
    curvature = precise(basis_panel.T, image_one)
    alpha_one = jnp.linalg.solve(curvature, gram_keys)
    residual_next = basis_panel - precise(image_one, alpha_one)
    norm_next = precise(residual_next.T, residual_next)
    beta_one = jnp.linalg.solve(gram_keys, norm_next)
    direction = residual_next + precise(basis_panel, beta_one)
    key_direction = precise(key_rows, direction)
    curvature_two = precise(direction.T, precise(covariance, direction)) + precise(key_direction.T, key_direction)
    alpha_two = jnp.linalg.solve(curvature_two, norm_next)
    solved = precise(basis_panel, alpha_one) + precise(direction, alpha_two)
    return precise(solved, residual)
```

```python
import jax
import jax.numpy as jnp
from jax import lax
from jax.experimental import pallas as pl
from jax.experimental.pallas import tpu as pltpu
from jax.sharding import PartitionSpec as P

VMEM_LIMIT = 56 * 2**20
LANES = 128
ACROSS = (((1,), (1,)), ((), ()))
PLAIN = (((1,), (0,)), ((), ()))


def tile_of(extent, most):
    best = extent
    for tile in range(LANES, min(extent, most) + 1, LANES):
        if extent % tile == 0:
            best = tile
    return best


def split(value):
    high = value.astype(jnp.bfloat16)
    return high, (value - high.astype(jnp.float32)).astype(jnp.bfloat16)


def precise(left, right, dims=PLAIN):
    return lax.dot_general(
        left, right, dims, precision=lax.Precision.HIGHEST, preferred_element_type=jnp.float32
    )


def split_product(both, right, dims):
    count = both.shape[0] // 2
    high, low = split(right)
    wide = lax.dot_general(both, high, dims, preferred_element_type=jnp.float32)
    rest = lax.dot_general(both[:count], low, dims, preferred_element_type=jnp.float32)
    return wide[:count] + wide[count:] + rest


def settings(flops, moved):
    return dict(
        compiler_params=pltpu.CompilerParams(vmem_limit_bytes=VMEM_LIMIT),
        cost_estimate=pl.CostEstimate(flops=flops, bytes_accessed=moved, transcendentals=0),
    )


def floats(*shape):
    return jax.ShapeDtypeStruct(shape, jnp.float32)


def image_kernel(places_ref, keys_ref, block_ref, out_ref, both):
    count, depth = keys_ref.shape

    @pl.when(pl.program_id(0) == 0)
    def _():
        both[:count], both[count:] = split(keys_ref[...])

    step = tile_of(depth, 640)
    total = jnp.zeros(out_ref.shape[1:], jnp.float32)
    for start in range(0, depth, step):
        part = slice(start, start + step)
        total = total + split_product(both[:, part], block_ref[part, :], PLAIN)
    out_ref[0] = total


def image_pieces(keys, covariance, places, width):
    count, depth = keys.shape
    pieces = places.shape[0]
    if width % LANES:
        step = tile_of(covariance.shape[1], 640)
        full = image_pieces(
            keys, covariance, jnp.arange(covariance.shape[1] // step, dtype=jnp.int32), step
        )
        full = full.transpose(1, 0, 2).reshape(count, -1)
        return jnp.stack(
            [lax.dynamic_slice_in_dim(full, places[i] * width, width, 1) for i in range(pieces)]
        )
    return pl.pallas_call(
        image_kernel,
        out_shape=floats(pieces, count, width),
        grid_spec=pltpu.PrefetchScalarGridSpec(
            num_scalar_prefetch=1,
            grid=(pieces,),
            in_specs=[
                pl.BlockSpec((count, depth), lambda j, places: (0, 0)),
                pl.BlockSpec((depth, width), lambda j, places: (0, places[j])),
            ],
            out_specs=pl.BlockSpec((1, count, width), lambda j, places: (j, 0, 0)),
            scratch_shapes=[pltpu.VMEM((2 * count, depth), jnp.bfloat16)],
        ),
        **settings(6 * count * depth * width * pieces, 4 * depth * width * pieces),
    )(places, keys, covariance)


def apply_kernel(places_ref, order_ref, piece_ref, block_ref, *rest):
    *before, out_ref, both = rest
    count, width = piece_ref.shape[1:]
    shares, _, rows = out_ref.shape

    @pl.when(pl.program_id(0) == 0)
    def _():
        out_ref[...] = before[0][...] if before else jnp.zeros(out_ref.shape, jnp.float32)

    both[:count], both[count:] = split(piece_ref[0])
    for share in range(shares):
        start = pl.multiple_of(order_ref[share] * rows, 8)
        out_ref[share] += split_product(both[...], block_ref[pl.ds(start, rows), :], ACROSS)


def apply_pieces(pieces, covariance, places, order, before=None):
    number, count, width = pieces.shape
    depth, shares = covariance.shape[0], order.shape[0]
    rows = depth // shares
    if width % LANES:
        step = tile_of(covariance.shape[1], 640)
        full = jnp.zeros((count, covariance.shape[1]), jnp.float32)
        for i in range(number):
            full = lax.dynamic_update_slice_in_dim(full, pieces[i], places[i] * width, 1)
        full = full.reshape(count, -1, step).transpose(1, 0, 2)
        return apply_pieces(
            full, covariance, jnp.arange(full.shape[0], dtype=jnp.int32), order, before
        )
    whole = pl.BlockSpec((shares, count, rows), lambda j, places, order: (0, 0, 0))
    extra = [] if before is None else [before]
    return pl.pallas_call(
        apply_kernel,
        out_shape=floats(shares, count, rows),
        grid_spec=pltpu.PrefetchScalarGridSpec(
            num_scalar_prefetch=2,
            grid=(number,),
            in_specs=[
                pl.BlockSpec((1, count, width), lambda j, places, order: (j, 0, 0)),
                pl.BlockSpec((depth, width), lambda j, places, order: (0, places[j])),
                *[whole for _ in extra],
            ],
            out_specs=whole,
            scratch_shapes=[pltpu.VMEM((2 * count, width), jnp.bfloat16)],
        ),
        **settings(6 * count * depth * width * number, 4 * depth * width * number),
    )(places, order, pieces, covariance, *extra)


def fitted_kernel(places_ref, keys_ref, weight_ref, theirs_ref, mine_ref, sorted_keys, both):
    count = keys_ref.shape[0]
    pieces = places_ref.shape[0]
    rows, half = count // pieces, count // 2

    @pl.when(pl.program_id(0) == 0)
    def _():
        for i in range(pieces):
            start = pl.multiple_of(places_ref[i] * rows, 8)
            sorted_keys[i * rows : (i + 1) * rows, :] = keys_ref[pl.ds(start, rows), :]
        both[:count], both[count:] = split(sorted_keys[...])

    total = split_product(both[...], weight_ref[...], PLAIN)
    theirs_ref[...], mine_ref[...] = total[:half], total[half:]


def fitted_parts(keys, weight, places):
    count, depth = keys.shape
    width = weight.shape[1]
    tile = tile_of(width, 256)
    half = pl.BlockSpec((count // 2, tile), lambda j, places: (0, j))
    return pl.pallas_call(
        fitted_kernel,
        out_shape=[floats(count // 2, width)] * 2,
        grid_spec=pltpu.PrefetchScalarGridSpec(
            num_scalar_prefetch=1,
            grid=(width // tile,),
            in_specs=[
                pl.BlockSpec((count, depth), lambda j, places: (0, 0)),
                pl.BlockSpec((depth, tile), lambda j, places: (0, j)),
            ],
            out_specs=[half, half],
            scratch_shapes=[
                pltpu.VMEM((count, depth), jnp.float32),
                pltpu.VMEM((2 * count, depth), jnp.bfloat16),
            ],
        ),
        **settings(6 * count * depth * width, 4 * depth * width),
    )(places, keys, weight)


def moments_kernel(col_ref, keys_ref, piece_ref, share_ref, out_ref):
    width = share_ref.shape[1]
    out_ref[0] = precise(keys_ref[...], keys_ref[...], ACROSS)
    for i in range(keys_ref.shape[1] // width):

        @pl.when(col_ref[0] == i)
        def _():
            part = keys_ref[:, i * width : (i + 1) * width]
            out_ref[1] = precise(part, share_ref[...], ACROSS)

    out_ref[2] = precise(piece_ref[...], piece_ref[...], ACROSS)


def moments(keys, piece, share, col):
    count = keys.shape[0]
    return pl.pallas_call(
        moments_kernel,
        out_shape=floats(3, count, count),
        in_specs=[pl.BlockSpec(memory_space=pltpu.SMEM)]
        + [pl.BlockSpec(memory_space=pltpu.VMEM)] * 3,
        out_specs=pl.BlockSpec(memory_space=pltpu.VMEM),
        **settings(12 * count * count * keys.shape[1], 8 * keys.size),
    )(col.reshape(1), keys, piece, share)


def third_kernel(image_ref, *refs):
    *shares, out_ref = refs
    out_ref[...] = sum(
        precise(share[...], image_ref[i], ACROSS) for i, share in enumerate(shares)
    )


def third_moment(shares, image):
    count = image.shape[1]
    return pl.pallas_call(
        third_kernel,
        out_shape=floats(count, count),
        **settings(12 * count * image.size, 8 * image.size),
    )(image, *shares)


def eliminate(work, count):
    row = lax.broadcasted_iota(jnp.int32, (count, 1), 0)
    for k in range(count):
        pivot_row = work[k : k + 1, :]
        scaled = pivot_row * (1.0 / pivot_row[:, k : k + 1])
        factor = jnp.where(row == k, 0.0, work[:, k : k + 1])
        updated = work[...] - factor * scaled
        work[...] = jnp.where(row == k, scaled, updated)


def early_kernel(gram_ref, moments_ref, alpha_ref, basis_ref, right_ref, known_ref, work):
    count = gram_ref.shape[0]
    gram, first, second = gram_ref[...], moments_ref[0], moments_ref[1]
    first = 0.5 * (first + first.T)
    curvature = first + precise(gram, gram)
    three = precise(gram, jnp.concatenate([first, second, curvature], axis=1))
    gram_first, gram_second, gram_curvature = (
        three[:, i * count : (i + 1) * count] for i in range(3)
    )
    square = second + gram_first.T + gram_curvature
    work[:, :count] = 0.5 * (curvature + curvature.T)
    work[:, count : 2 * count] = square
    work[:, 2 * count :] = gram
    eliminate(work, count)
    moved, alpha = work[:, count : 2 * count], work[:, 2 * count :]
    two = precise(square, work[:, count:])
    alpha_ref[...] = alpha
    basis_ref[...] = gram - moved
    right_ref[...] = curvature - two[:, count:]
    known_ref[...] = (
        gram_second
        + gram_second.T
        + precise(gram_first, gram)
        + precise(curvature, curvature)
        - two[:, :count]
    )


def early_solve(gram, pair):
    count = gram.shape[0]
    return pl.pallas_call(
        early_kernel,
        out_shape=[floats(count, count)] * 4,
        scratch_shapes=[pltpu.VMEM((count, 3 * count), jnp.float32)],
        **settings(60 * count**3, 32 * count**2),
    )(gram, pair)


def late_kernel(
    places_ref, third_ref, known_ref, right_ref, alpha_ref, basis_ref, theirs_ref, mine_ref,
    targets_ref, high_ref, low_ref, work, residual,
):
    count = third_ref.shape[0]
    pieces = places_ref.shape[0]
    rows, half = count // pieces, count // 2
    for i in range(pieces):
        start = pl.multiple_of(places_ref[i] * rows, 8)
        source, at = (theirs_ref, i * rows) if i * rows < half else (mine_ref, i * rows - half)
        part = pl.ds(start, rows)
        residual[part, :] = targets_ref[part, :] - source[at : at + rows, :]
    matrix = third_ref[...] + known_ref[...]
    work[:, :count] = 0.5 * (matrix + matrix.T)
    work[:, count:] = right_ref[...]
    eliminate(work, count)
    lower = precise(work[:, count:], residual[...])
    upper = precise(alpha_ref[...], residual[...]) + precise(basis_ref[...], lower)
    high_ref[:count], low_ref[:count] = split(upper)
    high_ref[count:], low_ref[count:] = split(lower)


def late_solve(third, known, right, alpha, basis, theirs, mine, targets, places):
    count, width = targets.shape
    halves = jax.ShapeDtypeStruct((2 * count, width), jnp.bfloat16)
    return pl.pallas_call(
        late_kernel,
        out_shape=[halves, halves],
        in_specs=[pl.BlockSpec(memory_space=pltpu.SMEM)]
        + [pl.BlockSpec(memory_space=pltpu.VMEM)] * 8,
        scratch_shapes=[
            pltpu.VMEM((count, 2 * count), jnp.float32),
            pltpu.VMEM((count, width), jnp.float32),
        ],
        **settings(40 * count**3, 16 * count * width),
    )(places, third, known, right, alpha, basis, theirs, mine, targets)


def upright_kernel(order_ref, keys_ref, *refs):
    *shares, high_ref, low_ref = refs
    count = keys_ref.shape[0]
    high_ref[:, :count], low_ref[:, :count] = split(keys_ref[...].T)
    for i, share in enumerate(shares):
        rows = share.shape[1]
        part = pl.ds(pl.multiple_of(order_ref[i] * rows, 16), rows)
        high_ref[part, count:], low_ref[part, count:] = split(share[...].T)


def upright(keys, shares, order):
    count, depth = keys.shape
    tall = jax.ShapeDtypeStruct((depth, 2 * count), jnp.bfloat16)
    return pl.pallas_call(
        upright_kernel,
        out_shape=[tall, tall],
        in_specs=[pl.BlockSpec(memory_space=pltpu.SMEM)]
        + [pl.BlockSpec(memory_space=pltpu.VMEM)] * (1 + len(shares)),
        **settings(count * depth, 16 * count * depth),
    )(order, keys, *shares)


def increment_kernel(high_ref, low_ref, right_high_ref, right_low_ref, out_ref):
    out_ref[...] = (
        jnp.dot(high_ref[...], right_high_ref[...], preferred_element_type=jnp.float32)
        + jnp.dot(low_ref[...], right_high_ref[...], preferred_element_type=jnp.float32)
        + jnp.dot(high_ref[...], right_low_ref[...], preferred_element_type=jnp.float32)
    )


def increment_product(high, low, right_high, right_low):
    rows, depth = high.shape
    width = right_high.shape[1]
    tile = tile_of(rows, 256)
    left = pl.BlockSpec((tile, depth), lambda j: (j, 0))
    right = pl.BlockSpec((depth, width), lambda j: (0, 0))
    return pl.pallas_call(
        increment_kernel,
        out_shape=floats(rows, width),
        grid=(rows // tile,),
        in_specs=[left, left, right, right],
        out_specs=pl.BlockSpec((tile, width), lambda j: (j, 0)),
        **settings(6 * depth * rows * width, 4 * (depth * rows + depth * width + rows * width)),
    )(high, low, right_high, right_low)


def swap(value, mask):
    return lax.ppermute(value, "row", [(i, i ^ mask) for i in range(lax.axis_size("row"))])


def others(value):
    count = lax.axis_size("col")
    return [
        lax.ppermute(value, "col", [(i, (i + d) % count) for i in range(count)])
        for d in range(1, count)
    ]


def chip_masks():
    return range(2, lax.axis_size("row"), 2)


def sum_over_row(value):
    value = value + swap(value, 1)
    return sum((swap(value, mask) for mask in chip_masks()), value)


def sum_over_col(value):
    return sum(others(value), value)


def after(value, *earlier):
    return lax.optimization_barrier((value, *earlier))[0]


def to_rows(value, k):
    rows, cols = lax.axis_size("row"), lax.axis_size("col")
    blocks, chips = rows // cols, rows // 2
    pairs = []
    for row in range(rows):
        place = (row % 2) * chips + row // 2
        for col in range(cols):
            target = (blocks * col + place // cols) * cols + (place % cols - k) % cols
            pairs.append((row * cols + col, target))
    return lax.ppermute(value, ("row", "col"), pairs)


def body(key_rows, targets, weight, covariance):
    rows, cols = lax.axis_size("row"), lax.axis_size("col")
    row, col = lax.axis_index("row"), lax.axis_index("col")
    chips, core, chip = rows // 2, row % 2, row // 2
    count = key_rows.shape[0] * cols
    width = covariance.shape[1] // rows
    near = jnp.bitwise_xor(jnp.arange(chips, dtype=jnp.int32), chip)
    mine, theirs = core * chips + near, (1 - core) * chips + near
    order = (col + jnp.arange(cols, dtype=jnp.int32)) % cols

    keys = jnp.zeros((cols, *key_rows.shape), key_rows.dtype)
    for d, block in enumerate([key_rows, *others(key_rows)]):
        keys = lax.dynamic_update_index_in_dim(keys, block, (col - d) % cols, 0)
    keys = keys.reshape(count, -1)

    far_part = image_pieces(keys, covariance, theirs, width)
    near_part = image_pieces(after(keys, far_part), covariance, mine, width)
    part = near_part + swap(far_part, 1)
    piece = sum((swap(part[mask // 2], mask) for mask in chip_masks()), part[0])

    fitted_theirs, fitted_mine = fitted_parts(
        after(keys, near_part), weight, jnp.concatenate([theirs, mine])
    )

    near_pieces = jnp.stack([piece, *[swap(piece, mask) for mask in chip_masks()]])
    shares = [to_rows(piece, k) for k in range(cols)]
    far_pieces = swap(near_pieces, 1)

    fitted = fitted_mine + swap(fitted_theirs, 1)
    height = count // rows
    fitted = fitted.reshape(chips, height, -1)
    fitted = sum((swap(fitted[mask // 2], mask) for mask in chip_masks()), fitted[0])
    fitted_mine = jnp.concatenate([fitted, *[swap(fitted, mask) for mask in chip_masks()]], axis=0)
    fitted_theirs = swap(fitted_mine, 1)

    sums = sum_over_row(moments(keys, piece, shares[0], col))
    gram, pair = sums[0], sum_over_col(sums[1:])
    alpha, basis, right, known = early_solve(gram, pair)

    applied = apply_pieces(near_pieces, covariance, mine, order)
    applied = apply_pieces(far_pieces, covariance, theirs, order, applied)
    third = sum_over_col(sum_over_row(third_moment(shares, applied)))
    tall_high, tall_low = upright(keys, shares, order)

    high, low = late_solve(
        third, known, right, alpha, basis, fitted_theirs, fitted_mine, targets,
        jnp.concatenate([theirs, mine]),
    )
    return increment_product(tall_high, tall_low, high, low)


def solution(mesh):
    placed = (P("col", "row"), P(None, "col"), P("row", "col"), P("row", "col"))
    return jax.shard_map(
        body, mesh=mesh, in_specs=placed, out_specs=P("row", "col"), check_vma=False
    )
```

```python
import functools

import jax
import jax.numpy as jnp
from jax import lax
from jax.experimental import pallas as pl
from jax.experimental.pallas import tpu as pltpu
from jax.sharding import PartitionSpec as P

VMEM_LIMIT = 56 * 2**20
STEP = 1280
COVER = 64
IMAGE_ROWS, IMAGE_SLOTS = 1280, 4
APPLY_ROWS, APPLY_SLOTS = 1280, 4
WEIGHT_ROWS, WEIGHT_SLOTS = 512, 5
APPLY_STEP = 1280
LANES = 128
ACROSS = (((1,), (1,)), ((), ()))
PLAIN = (((1,), (0,)), ((), ()))


def tile_of(extent, most):
    best = extent
    for tile in range(LANES, min(extent, most) + 1, LANES):
        if extent % tile == 0:
            best = tile
    return best


def split(value):
    high = value.astype(jnp.bfloat16)
    return high, (value - high.astype(jnp.float32)).astype(jnp.bfloat16)


def precise(left, right, dims=PLAIN):
    return lax.dot_general(
        left, right, dims, precision=lax.Precision.HIGHEST, preferred_element_type=jnp.float32
    )


def split_product(both, right, dims):
    count = both.shape[0] // 2
    high, low = split(right)
    wide = lax.dot_general(both, high, dims, preferred_element_type=jnp.float32)
    rest = lax.dot_general(both[:count], low, dims, preferred_element_type=jnp.float32)
    return wide[:count] + wide[count:] + rest


def triple(left, right, dims=PLAIN):
    high, low = split(left)
    return split_product(jnp.concatenate([high, low], axis=0), right, dims)


def settings(flops, moved):
    return dict(
        compiler_params=pltpu.CompilerParams(vmem_limit_bytes=VMEM_LIMIT),
        cost_estimate=pl.CostEstimate(
            flops=flops // COVER, bytes_accessed=moved // COVER, transcendentals=0
        ),
    )


def floats(*shape):
    return jax.ShapeDtypeStruct(shape, jnp.float32)


def chunk_rows(depth, rows, first):
    marks = list(range(0, depth, rows)) + [depth]
    if first and STEP < marks[1] and marks[1] % STEP == 0:
        marks.insert(1, STEP)
    return list(zip(marks, marks[1:]))


def stream(source, slices, slots, semaphores, use):
    number = slots.shape[0]
    copies = [
        pltpu.make_async_copy(
            source.at[part], slots.at[t % number, pl.ds(0, part[0].size)], semaphores.at[t % number]
        )
        for t, part in enumerate(slices)
    ]
    for copy in copies[:number]:
        copy.start()
    for t, copy in enumerate(copies):
        copy.wait()
        use(t, slots.at[t % number])
        if t + number < len(copies):
            copies[t + number].start()


def image_kernel(places_ref, keys_ref, source_ref, *rest, part, rows, offset):
    *before, out_ref, both, slots, semaphores = rest
    count, depth = keys_ref.shape
    number, _, width = out_ref.shape
    slot_count, _, tile = slots.shape
    per = tile // width
    slices, marks = [], []
    for group in range(0, number, per):
        start = pl.multiple_of(places_ref[group] // per * tile, LANES)
        for at, end in chunk_rows(depth, rows, group == 0):
            slices.append((pl.ds(part * depth + at, end - at), pl.ds(start, tile)))
            marks.append((group, at, end))
    totals = {}

    def use(t, slot):
        if t == 0:
            both[:count], both[count:] = split(keys_ref[...])
        group, at, end = marks[t]
        step = tile_of(end - at, STEP)
        for low in range(at, end, step):
            found = split_product(
                both[:, low : low + step], slot[low - at : low - at + step, :], PLAIN
            )
            totals[group] = totals[group] + found if group in totals else found
        if end == depth:
            found = totals.pop(group)
            for i in range(per):
                target = group + jnp.bitwise_xor(places_ref[0] % per, i)
                value = found[:, i * width : (i + 1) * width]
                out_ref[target] = value + before[0][offset + target] if before else value

    stream(source_ref, slices, slots, semaphores, use)


def paired(width):
    return 2 * width if width % (2 * LANES) else width


def image_pieces(keys, covariance, places, width, part, before=None, offset=0):
    count, depth = keys.shape
    pieces = places.shape[0]
    if width % LANES:
        step = tile_of(covariance.shape[1], 640)
        blocks = jnp.arange(covariance.shape[1] // step, dtype=jnp.int32)
        full = image_pieces(keys, covariance, blocks, step, part)
        full = full.transpose(1, 0, 2).reshape(count, -1)
        found = jnp.stack(
            [lax.dynamic_slice_in_dim(full, places[i] * width, width, 1) for i in range(pieces)]
        )
        return found if before is None else found + before[offset : offset + pieces]
    tile, rows = paired(width), tile_of(depth, IMAGE_ROWS)
    extra = [] if before is None else [before]
    return pl.pallas_call(
        functools.partial(image_kernel, part=part, rows=rows, offset=offset),
        out_shape=floats(pieces, count, width),
        in_specs=[
            pl.BlockSpec(memory_space=pltpu.SMEM),
            pl.BlockSpec(memory_space=pltpu.VMEM),
            pl.BlockSpec(memory_space=pl.ANY),
            *[pl.BlockSpec(memory_space=pltpu.VMEM) for _ in extra],
        ],
        scratch_shapes=[
            pltpu.VMEM((2 * count, depth), jnp.bfloat16),
            pltpu.VMEM((IMAGE_SLOTS, rows, tile), jnp.float32),
            pltpu.SemaphoreType.DMA((IMAGE_SLOTS,)),
        ],
        **settings(6 * count * depth * width * pieces, 4 * depth * width * pieces),
    )(places, keys, covariance, *extra)


def apply_kernel(places_ref, pieces_ref, source_ref, *rest, number, offset):
    *before, out_ref, both, slots, semaphores = rest
    _, count, width = pieces_ref.shape
    slot_count, rows, tile = slots.shape
    per = tile // width
    depth = source_ref.shape[0]
    slices, marks = [], []
    for group in range(0, number, per):
        start = pl.multiple_of(places_ref[offset + group] // per * tile, LANES)
        for at, end in chunk_rows(depth, rows, group == 0):
            slices.append((pl.ds(at, end - at), pl.ds(start, tile)))
            marks.append((group, at, end))

    def use(t, slot):
        group, at, end = marks[t]
        if at == 0:
            for i in range(per):
                piece = pieces_ref[offset + group + jnp.bitwise_xor(places_ref[0] % per, i)].T
                part = slice(i * width, (i + 1) * width)
                both[part, :count], both[part, count:] = split(piece)
        step = tile_of(end - at, APPLY_STEP)
        for low in range(at, end, step):
            high, rest = split(slot[low - at : low - at + step, :])
            wide = lax.dot_general(high, both[...], PLAIN, preferred_element_type=jnp.float32)
            rest = lax.dot_general(
                rest, both[:, :count], PLAIN, preferred_element_type=jnp.float32
            )
            found = wide[:, :count] + wide[:, count:] + rest
            part = slice(low, low + step)
            if group:
                out_ref[part] += found
            else:
                out_ref[part] = found + before[0][part] if before else found

    stream(source_ref, slices, slots, semaphores, use)


def apply_pieces(pieces, covariance, places, before=None, offset=0, number=None):
    total, count, width = pieces.shape
    number = number or total
    depth = covariance.shape[0]
    if width % LANES:
        step = tile_of(covariance.shape[1], 640)
        full = jnp.zeros((count, covariance.shape[1]), jnp.float32)
        for i in range(offset, offset + number):
            full = lax.dynamic_update_slice_in_dim(full, pieces[i], places[i] * width, 1)
        full = full.reshape(count, -1, step).transpose(1, 0, 2)
        blocks = jnp.arange(full.shape[0], dtype=jnp.int32)
        return apply_pieces(full, covariance, blocks, before)
    tile, rows = paired(width), tile_of(depth, APPLY_ROWS)
    extra = [] if before is None else [before]
    return pl.pallas_call(
        functools.partial(apply_kernel, number=number, offset=offset),
        out_shape=floats(depth, count),
        in_specs=[
            pl.BlockSpec(memory_space=pltpu.SMEM),
            pl.BlockSpec(memory_space=pltpu.VMEM),
            pl.BlockSpec(memory_space=pl.ANY),
            *[pl.BlockSpec(memory_space=pltpu.VMEM) for _ in extra],
        ],
        scratch_shapes=[
            pltpu.VMEM((tile, 2 * count), jnp.bfloat16),
            pltpu.VMEM((APPLY_SLOTS, rows, tile), jnp.float32),
            pltpu.SemaphoreType.DMA((APPLY_SLOTS,)),
        ],
        **settings(6 * count * depth * width * number, 4 * depth * width * number),
    )(places, pieces, covariance, *extra)


def fitted_kernel(places_ref, keys_ref, source_ref, far_ref, near_ref, both, sorted_keys, slots, semaphores):
    count, depth = keys_ref.shape
    _, rows, width = slots.shape
    half = count // 2
    height = count // places_ref.shape[0]
    marks = chunk_rows(depth, rows, True)
    slices = [(pl.ds(at, end - at), pl.ds(0, width)) for at, end in marks]

    def use(t, slot):
        if t == 0:
            for i in range(count // height):
                start = pl.multiple_of(places_ref[i] * height, 8)
                sorted_keys[i * height : (i + 1) * height, :] = keys_ref[pl.ds(start, height), :]
            both[:count], both[count:] = split(sorted_keys[...])
        at, end = marks[t]
        found = split_product(both[:, at:end], slot[: end - at, :], PLAIN)
        far_ref[...] = far_ref[...] + found[:half] if t else found[:half]
        near_ref[...] = near_ref[...] + found[half:] if t else found[half:]

    stream(source_ref, slices, slots, semaphores, use)


def fitted_part(keys, weight, places):
    count, depth = keys.shape
    width = weight.shape[1]
    rows = tile_of(depth, WEIGHT_ROWS)
    return pl.pallas_call(
        fitted_kernel,
        out_shape=[floats(count // 2, width)] * 2,
        in_specs=[
            pl.BlockSpec(memory_space=pltpu.SMEM),
            pl.BlockSpec(memory_space=pltpu.VMEM),
            pl.BlockSpec(memory_space=pl.ANY),
        ],
        scratch_shapes=[
            pltpu.VMEM((2 * count, depth), jnp.bfloat16),
            pltpu.VMEM((count, depth), jnp.float32),
            pltpu.VMEM((WEIGHT_SLOTS, rows, width), jnp.float32),
            pltpu.SemaphoreType.DMA((WEIGHT_SLOTS,)),
        ],
        **settings(6 * count * depth * width, 4 * depth * width),
    )(places, keys, weight)


def moments_kernel(col_ref, keys_ref, piece_ref, share_ref, out_ref):
    width = share_ref.shape[1]
    for i in range(keys_ref.shape[1] // width):

        @pl.when(col_ref[0] == i)
        def _():
            part = keys_ref[:, i * width : (i + 1) * width]
            out_ref[0] = precise(part, share_ref[...], ACROSS)

    out_ref[1] = precise(piece_ref[...], piece_ref[...], ACROSS)
    out_ref[2] = precise(keys_ref[...], keys_ref[...], ACROSS)


def moments(keys, piece, share, col):
    count = keys.shape[0]
    return pl.pallas_call(
        moments_kernel,
        out_shape=floats(3, count, count),
        in_specs=[pl.BlockSpec(memory_space=pltpu.SMEM)]
        + [pl.BlockSpec(memory_space=pltpu.VMEM)] * 3,
        out_specs=pl.BlockSpec(memory_space=pltpu.VMEM),
        **settings(12 * count * count * keys.shape[1], 8 * keys.size),
    )(col.reshape(1), keys, piece, share)


def third_kernel(order_ref, image_ref, *refs):
    *shares, out_ref = refs
    total = jnp.zeros(out_ref.shape, jnp.float32)
    for i, share in enumerate(shares):
        rows = share.shape[1]
        part = image_ref[pl.ds(pl.multiple_of(order_ref[i] * rows, 8), rows), :]
        total = total + precise(share[...], part)
    out_ref[...] = total


def third_moment(shares, image, order):
    count = image.shape[1]
    return pl.pallas_call(
        third_kernel,
        out_shape=floats(count, count),
        in_specs=[pl.BlockSpec(memory_space=pltpu.SMEM)]
        + [pl.BlockSpec(memory_space=pltpu.VMEM)] * (1 + len(shares)),
        **settings(12 * count * image.size, 8 * image.size),
    )(order, image, *shares)


def invert_block(entries, size):
    def entry(i, j):
        return entries[min(i, j), max(i, j)]

    for k in range(size):
        inverse = 1.0 / entry(k, k)
        scaled = [entry(i, k) * inverse for i in range(size)]
        updated = {}
        for i in range(size):
            for j in range(i, size):
                if i != k and j != k:
                    updated[i, j] = entries[i, j] - entry(i, k) * scaled[j]
                elif i == j:
                    updated[i, j] = -inverse
                else:
                    updated[i, j] = scaled[j if i == k else i]
        entries = updated
    return {key: -value for key, value in entries.items()}


def eliminate(work, count, block=8):
    row = lax.broadcasted_iota(jnp.int32, (count, count), 0)
    lane = lax.broadcasted_iota(jnp.int32, (count, count), 1)
    matrix = work[:, :count]
    diagonal = jnp.where(row == lane, matrix, 0.0)
    across = lax.rsqrt(jnp.sum(diagonal, axis=0, keepdims=True))
    down = lax.rsqrt(jnp.sum(diagonal, axis=1, keepdims=True))
    work[:, :count] = matrix * down * across
    work[:, count:] = work[:, count:] * down
    width = work.shape[1]
    for at in range(0, count, block):
        panel = work[at : at + block, :]
        entries = {
            (i, j): jnp.broadcast_to(panel[i : i + 1, at + j : at + j + 1], (1, LANES))
            for i in range(block)
            for j in range(i, block)
        }
        entries = invert_block(entries, block)
        solved = 0.0
        for j in range(block):
            column = jnp.concatenate(
                [entries[min(i, j), max(i, j)] for i in range(block)], axis=0
            )
            column = jnp.concatenate([column] * (width // LANES), axis=1)
            solved = solved + column * panel[j : j + 1, :]
        columns = work[:, at : at + block]
        updated = work[...]
        for j in range(block):
            updated = updated - columns[:, j : j + 1] * solved[j : j + 1, :]
        work[...] = updated
        work[at : at + block, :] = solved
    return work[:, count:] * down


def early_kernel(gram_ref, moments_ref, alpha_ref, basis_ref, right_ref, known_ref, work):
    count = gram_ref.shape[0]
    gram, first, second = gram_ref[...], moments_ref[0], moments_ref[1]
    first = 0.5 * (first + first.T)
    curvature = first + precise(gram, gram)
    curvature = 0.5 * (curvature + curvature.T)
    three = precise(gram, jnp.concatenate([first, second, curvature], axis=1))
    gram_first, gram_second, gram_curvature = (
        three[:, i * count : (i + 1) * count] for i in range(3)
    )
    square = second + gram_first.T + gram_curvature
    work[:, :count], work[:, count : 2 * count], work[:, 2 * count :] = curvature, square, gram
    solved = eliminate(work, count)
    two = precise(square, solved)
    alpha_ref[...] = solved[:, count:]
    basis_ref[...] = gram - solved[:, :count]
    right_ref[...] = curvature - two[:, count:]
    known_ref[...] = (
        gram_second
        + gram_second.T
        + precise(gram_first, gram)
        + precise(curvature, curvature)
        - two[:, :count]
    )


def early_solve(gram, pair):
    count = gram.shape[0]
    return pl.pallas_call(
        early_kernel,
        out_shape=[floats(count, count)] * 4,
        scratch_shapes=[pltpu.VMEM((count, 3 * count), jnp.float32)],
        **settings(60 * count**3, 32 * count**2),
    )(gram, pair)


def upright_kernel(order_ref, keys_ref, *refs):
    *shares, high_ref, low_ref = refs
    count = keys_ref.shape[0]
    high_ref[:, :count], low_ref[:, :count] = split(keys_ref[...].T)
    for i, share in enumerate(shares):
        rows = share.shape[1]
        part = pl.ds(pl.multiple_of(order_ref[i] * rows, 16), rows)
        high_ref[part, count:], low_ref[part, count:] = split(share[...].T)


def upright(keys, shares, order):
    count, depth = keys.shape
    tall = jax.ShapeDtypeStruct((depth, 2 * count), jnp.bfloat16)
    return pl.pallas_call(
        upright_kernel,
        out_shape=[tall, tall],
        in_specs=[pl.BlockSpec(memory_space=pltpu.SMEM)]
        + [pl.BlockSpec(memory_space=pltpu.VMEM)] * (1 + len(shares)),
        **settings(count * depth, 16 * count * depth),
    )(order, keys, *shares)


def increment_kernel(
    places_ref, third_ref, known_ref, right_ref, alpha_ref, basis_ref, targets_ref, fitted_ref,
    high_ref, low_ref,
    out_ref, right_high, right_low, work, residual,
):
    count = third_ref.shape[0]

    @pl.when(pl.program_id(0) == 0)
    def _():
        matrix = third_ref[...] + known_ref[...]
        work[:, :count], work[:, count:] = 0.5 * (matrix + matrix.T), right_ref[...]
        gamma = eliminate(work, count)
        height = count // places_ref.shape[0]
        for i in range(count // height):
            part = pl.ds(pl.multiple_of(places_ref[i] * height, 8), height)
            residual[part, :] = targets_ref[part, :] - fitted_ref[i * height : (i + 1) * height, :]
        lower = triple(gamma, residual[...])
        upper = triple(alpha_ref[...], residual[...]) + triple(basis_ref[...], lower)
        right_high[:count], right_low[:count] = split(upper)
        right_high[count:], right_low[count:] = split(lower)

    out_ref[...] = (
        jnp.dot(high_ref[...], right_high[...], preferred_element_type=jnp.float32)
        + jnp.dot(low_ref[...], right_high[...], preferred_element_type=jnp.float32)
        + jnp.dot(high_ref[...], right_low[...], preferred_element_type=jnp.float32)
    )


def increment_product(third, known, right, alpha, basis, targets, fitted, high, low, places):
    rows, depth = high.shape
    width = targets.shape[1]
    tile = tile_of(rows, 512)
    left = pl.BlockSpec((tile, depth), lambda j: (j, 0))
    square = pl.BlockSpec(third.shape, lambda j: (0, 0))
    return pl.pallas_call(
        increment_kernel,
        out_shape=floats(rows, width),
        grid=(rows // tile,),
        in_specs=[pl.BlockSpec(memory_space=pltpu.SMEM)]
        + [square] * 5
        + [pl.BlockSpec(targets.shape, lambda j: (0, 0))] * 2 + [left] * 2,
        out_specs=pl.BlockSpec((tile, width), lambda j: (j, 0)),
        scratch_shapes=[pltpu.VMEM((depth, width), jnp.bfloat16)] * 2
        + [pltpu.VMEM((third.shape[0], depth), jnp.float32), pltpu.VMEM(targets.shape, jnp.float32)],
        **settings(6 * depth * rows * width, 4 * (depth * rows + depth * width + rows * width)),
    )(places, third, known, right, alpha, basis, targets, fitted, high, low)


def swap(value, mask):
    return lax.ppermute(value, "row", [(i, i ^ mask) for i in range(lax.axis_size("row"))])


def others(value):
    count = lax.axis_size("col")
    return [
        lax.ppermute(value, "col", [(i, (i + d) % count) for i in range(count)])
        for d in range(1, count)
    ]


def chip_masks():
    return range(2, lax.axis_size("row"), 2)


def sum_over_row(value):
    value = value + swap(value, 1)
    return sum((swap(value, mask) for mask in chip_masks()), value)


def sum_over_col(value):
    return sum(others(value), value)


def row_masks():
    masks, order = [], [0]
    mask = 1
    while mask < lax.axis_size("row"):
        masks.append(mask)
        mask *= 2
    for mask in reversed(masks):
        order = order + [i | mask for i in order]
    return masks, order


def after(value, *earlier):
    return lax.optimization_barrier((value, *earlier))[0]


def to_rows(value, k):
    rows, cols = lax.axis_size("row"), lax.axis_size("col")
    blocks, chips = rows // cols, rows // 2
    pairs = []
    for row in range(rows):
        place = (row % 2) * chips + row // 2
        for col in range(cols):
            target = (blocks * col + place // cols) * cols + (place % cols - k) % cols
            pairs.append((row * cols + col, target))
    return lax.ppermute(value, ("row", "col"), pairs)


def body(key_rows, targets, weight, covariance):
    rows, cols = lax.axis_size("row"), lax.axis_size("col")
    row, col = lax.axis_index("row"), lax.axis_index("col")
    chips, core, chip = rows // 2, row % 2, row // 2
    count = key_rows.shape[0] * cols
    width = covariance.shape[1] // rows
    near = jnp.bitwise_xor(jnp.arange(chips, dtype=jnp.int32), chip)
    mine, theirs = core * chips + near, (1 - core) * chips + near
    places = jnp.concatenate([theirs, mine])
    masks, levels = row_masks()
    ranks = jnp.bitwise_xor(jnp.array(levels, dtype=jnp.int32), row)
    order = (col + jnp.arange(cols, dtype=jnp.int32)) % cols

    parts = 2 if key_rows.shape[1] % (2 * LANES) == 0 else 1
    depth = key_rows.shape[1] // parts
    sent, received = None, []
    for part in range(parts):
        block = key_rows[:, part * depth : (part + 1) * depth]
        received.append([block, *others(block if sent is None else after(block, *sent))])
        sent = received[-1][1:]
    key_parts, pieces = [], None
    for part in range(parts):
        keys = jnp.zeros((cols, key_rows.shape[0], depth), key_rows.dtype)
        for d, block in enumerate(received[part]):
            keys = lax.dynamic_update_index_in_dim(keys, block, (col - d) % cols, 0)
        key_parts.append(keys.reshape(count, -1))
        if part < parts - 1:
            pieces = image_pieces(key_parts[part], covariance, places, width, part, pieces)
    last = key_parts[-1]
    far_part = image_pieces(last, covariance, theirs, width, parts - 1, pieces)
    last = after(last, far_part)
    near_part = image_pieces(last, covariance, mine, width, parts - 1, pieces, chips)
    part = near_part + swap(far_part, 1)
    piece = sum((swap(part[mask // 2], mask) for mask in chip_masks()), part[0])

    keys = jnp.concatenate([after(block, part) for block in key_parts], axis=1)
    half = rows // 2
    fitted_far, fitted = fitted_part(keys, weight, jnp.concatenate([ranks[half:], ranks[:half]]))
    piece, fitted_far, fitted = lax.optimization_barrier((piece, fitted_far, fitted))
    near_pieces = jnp.stack([piece, *[swap(piece, mask) for mask in chip_masks()]])
    fitted = fitted + swap(fitted_far, 1)

    def halve(value, mask):
        keep = value.shape[0] // 2
        return value[:keep] + swap(value[keep:], mask)

    def double(value, mask):
        return jnp.concatenate([value, swap(value, mask)], axis=0)

    chain = [(halve, mask) for mask in masks[1:]] + [(double, mask) for mask in reversed(masks)]

    def advance(value, steps):
        for _ in range(steps):
            if chain:
                move, mask = chain.pop(0)
                value = move(value, mask)
        return value

    far_pieces = swap(near_pieces, 1)
    held = after(piece, near_pieces)
    shares = [to_rows(held, k) for k in range(cols - 1)]

    applied = apply_pieces(near_pieces, covariance, mine)
    sums = moments(keys, after(piece, applied), shares[0], col)
    far_pieces, applied, sums, *shares = lax.optimization_barrier(
        (far_pieces, applied, sums, *shares)
    )
    middle = max(chips // 2, 2)
    shares.append(to_rows(after(piece, *shares), cols - 1))
    sums = sums + swap(sums, 1)
    fitted = advance(fitted, 1)
    applied = apply_pieces(far_pieces, covariance, theirs, applied, 0, middle)
    applied, sums, fitted = lax.optimization_barrier((applied, sums, fitted))
    sums = sum((swap(sums, mask) for mask in chip_masks()), sums)
    fitted = advance(fitted, 1)
    if middle < chips:
        applied = apply_pieces(far_pieces, covariance, theirs, applied, middle, chips - middle)
    applied, sums, fitted = lax.optimization_barrier((applied, sums, fitted))
    gram = sums[2]

    pair = sum_over_col(sums[:2])
    third = third_moment(shares, applied, order)
    tall = upright(after(keys, third), shares, order)
    third = third + swap(third, 1)
    fitted = advance(fitted, 1)
    third, fitted, gram, pair, *tall = lax.optimization_barrier((third, fitted, gram, pair, *tall))
    third = sum((swap(third, mask) for mask in chip_masks()), third)
    fitted = advance(fitted, 1)
    early = early_solve(gram, pair)
    third, fitted, *early = lax.optimization_barrier((third, fitted, *early))
    third = sum_over_col(third)
    fitted = advance(fitted, len(chain))
    alpha, basis, right, known = early
    tall_high, tall_low = tall
    return increment_product(
        third, known, right, alpha, basis, targets, fitted, tall_high, tall_low, ranks
    )


def solution(mesh):
    placed = (P("col", "row"), P(None, "col"), P("row", "col"), P("row", "col"))
    return jax.shard_map(
        body, mesh=mesh, in_specs=placed, out_specs=P("row", "col"), check_vma=False
    )
```

```python
import functools

import jax
import jax.numpy as jnp
from jax import lax
from jax.experimental import pallas as pl
from jax.experimental.pallas import tpu as pltpu
from jax.sharding import PartitionSpec as P

VMEM_LIMIT = 56 * 2**20
STEP = 1280
COVER = 64
IMAGE_ROWS, IMAGE_SLOTS = 1280, 4
APPLY_ROWS, APPLY_SLOTS = 1280, 4
WEIGHT_ROWS, WEIGHT_SLOTS = 512, 5
APPLY_STEP = 1280
LANES = 128
ACROSS = (((1,), (1,)), ((), ()))
PLAIN = (((1,), (0,)), ((), ()))


def tile_of(extent, most):
    best = extent
    for tile in range(LANES, min(extent, most) + 1, LANES):
        if extent % tile == 0:
            best = tile
    return best


def split(value):
    high = value.astype(jnp.bfloat16)
    return high, (value - high.astype(jnp.float32)).astype(jnp.bfloat16)


def precise(left, right, dims=PLAIN):
    return lax.dot_general(
        left, right, dims, precision=lax.Precision.HIGHEST, preferred_element_type=jnp.float32
    )


def split_product(both, right, dims):
    count = both.shape[0] // 2
    high, low = split(right)
    wide = lax.dot_general(both, high, dims, preferred_element_type=jnp.float32)
    rest = lax.dot_general(both[:count], low, dims, preferred_element_type=jnp.float32)
    return wide[:count] + wide[count:] + rest


def triple(left, right, dims=PLAIN):
    high, low = split(left)
    return split_product(jnp.concatenate([high, low], axis=0), right, dims)


def settings(flops, moved):
    return dict(
        compiler_params=pltpu.CompilerParams(vmem_limit_bytes=VMEM_LIMIT),
        cost_estimate=pl.CostEstimate(
            flops=flops // COVER, bytes_accessed=moved // COVER, transcendentals=0
        ),
    )


def floats(*shape):
    return jax.ShapeDtypeStruct(shape, jnp.float32)


def chunk_rows(depth, rows, first):
    marks = list(range(0, depth, rows)) + [depth]
    if first and STEP < marks[1] and marks[1] % STEP == 0:
        marks.insert(1, STEP)
    return list(zip(marks, marks[1:]))


def stream(source, slices, slots, semaphores, use):
    number = slots.shape[0]
    copies = [
        pltpu.make_async_copy(
            source.at[part], slots.at[t % number, pl.ds(0, part[0].size)], semaphores.at[t % number]
        )
        for t, part in enumerate(slices)
    ]
    for copy in copies[:number]:
        copy.start()
    for t, copy in enumerate(copies):
        copy.wait()
        use(t, slots.at[t % number])
        if t + number < len(copies):
            copies[t + number].start()


def image_kernel(places_ref, keys_ref, source_ref, *rest, part, rows, offset):
    *before, out_ref, both, slots, semaphores = rest
    count, depth = keys_ref.shape
    number, _, width = out_ref.shape
    slot_count, _, tile = slots.shape
    per = tile // width
    slices, marks = [], []
    for group in range(0, number, per):
        start = pl.multiple_of(places_ref[group] // per * tile, LANES)
        for at, end in chunk_rows(depth, rows, group == 0):
            slices.append((pl.ds(part * depth + at, end - at), pl.ds(start, tile)))
            marks.append((group, at, end))
    totals = {}

    def use(t, slot):
        if t == 0:
            both[:count], both[count:] = split(keys_ref[...])
        group, at, end = marks[t]
        step = tile_of(end - at, STEP)
        for low in range(at, end, step):
            found = split_product(
                both[:, low : low + step], slot[low - at : low - at + step, :], PLAIN
            )
            totals[group] = totals[group] + found if group in totals else found
        if end == depth:
            found = totals.pop(group)
            for i in range(per):
                target = group + jnp.bitwise_xor(places_ref[0] % per, i)
                value = found[:, i * width : (i + 1) * width]
                out_ref[target] = value + before[0][offset + target] if before else value

    stream(source_ref, slices, slots, semaphores, use)


def paired(width):
    return 2 * width if width % (2 * LANES) else width


def image_pieces(keys, covariance, places, width, part, before=None, offset=0):
    count, depth = keys.shape
    pieces = places.shape[0]
    if width % LANES:
        step = tile_of(covariance.shape[1], 640)
        blocks = jnp.arange(covariance.shape[1] // step, dtype=jnp.int32)
        full = image_pieces(keys, covariance, blocks, step, part)
        full = full.transpose(1, 0, 2).reshape(count, -1)
        found = jnp.stack(
            [lax.dynamic_slice_in_dim(full, places[i] * width, width, 1) for i in range(pieces)]
        )
        return found if before is None else found + before[offset : offset + pieces]
    tile, rows = paired(width), tile_of(depth, IMAGE_ROWS)
    extra = [] if before is None else [before]
    return pl.pallas_call(
        functools.partial(image_kernel, part=part, rows=rows, offset=offset),
        out_shape=floats(pieces, count, width),
        in_specs=[
            pl.BlockSpec(memory_space=pltpu.SMEM),
            pl.BlockSpec(memory_space=pltpu.VMEM),
            pl.BlockSpec(memory_space=pl.ANY),
            *[pl.BlockSpec(memory_space=pltpu.VMEM) for _ in extra],
        ],
        scratch_shapes=[
            pltpu.VMEM((2 * count, depth), jnp.bfloat16),
            pltpu.VMEM((IMAGE_SLOTS, rows, tile), jnp.float32),
            pltpu.SemaphoreType.DMA((IMAGE_SLOTS,)),
        ],
        **settings(6 * count * depth * width * pieces, 4 * depth * width * pieces),
    )(places, keys, covariance, *extra)


def apply_kernel(places_ref, pieces_ref, source_ref, *rest, number, offset):
    *before, out_ref, both, slots, semaphores = rest
    _, count, width = pieces_ref.shape
    slot_count, rows, tile = slots.shape
    per = tile // width
    depth = source_ref.shape[0]
    slices, marks = [], []
    for group in range(0, number, per):
        start = pl.multiple_of(places_ref[offset + group] // per * tile, LANES)
        for at, end in chunk_rows(depth, rows, group == 0):
            slices.append((pl.ds(at, end - at), pl.ds(start, tile)))
            marks.append((group, at, end))

    def use(t, slot):
        group, at, end = marks[t]
        if at == 0:
            for i in range(per):
                piece = pieces_ref[offset + group + jnp.bitwise_xor(places_ref[0] % per, i)].T
                part = slice(i * width, (i + 1) * width)
                both[part, :count], both[part, count:] = split(piece)
        step = tile_of(end - at, APPLY_STEP)
        for low in range(at, end, step):
            high, rest = split(slot[low - at : low - at + step, :])
            wide = lax.dot_general(high, both[...], PLAIN, preferred_element_type=jnp.float32)
            rest = lax.dot_general(
                rest, both[:, :count], PLAIN, preferred_element_type=jnp.float32
            )
            found = wide[:, :count] + wide[:, count:] + rest
            part = slice(low, low + step)
            if group:
                out_ref[part] += found
            else:
                out_ref[part] = found + before[0][part] if before else found

    stream(source_ref, slices, slots, semaphores, use)


def apply_pieces(pieces, covariance, places, before=None, offset=0, number=None):
    total, count, width = pieces.shape
    number = number or total
    depth = covariance.shape[0]
    if width % LANES:
        step = tile_of(covariance.shape[1], 640)
        full = jnp.zeros((count, covariance.shape[1]), jnp.float32)
        for i in range(offset, offset + number):
            full = lax.dynamic_update_slice_in_dim(full, pieces[i], places[i] * width, 1)
        full = full.reshape(count, -1, step).transpose(1, 0, 2)
        blocks = jnp.arange(full.shape[0], dtype=jnp.int32)
        return apply_pieces(full, covariance, blocks, before)
    tile, rows = paired(width), tile_of(depth, APPLY_ROWS)
    extra = [] if before is None else [before]
    return pl.pallas_call(
        functools.partial(apply_kernel, number=number, offset=offset),
        out_shape=floats(depth, count),
        in_specs=[
            pl.BlockSpec(memory_space=pltpu.SMEM),
            pl.BlockSpec(memory_space=pltpu.VMEM),
            pl.BlockSpec(memory_space=pl.ANY),
            *[pl.BlockSpec(memory_space=pltpu.VMEM) for _ in extra],
        ],
        scratch_shapes=[
            pltpu.VMEM((tile, 2 * count), jnp.bfloat16),
            pltpu.VMEM((APPLY_SLOTS, rows, tile), jnp.float32),
            pltpu.SemaphoreType.DMA((APPLY_SLOTS,)),
        ],
        **settings(6 * count * depth * width * number, 4 * depth * width * number),
    )(places, pieces, covariance, *extra)


def fitted_kernel(places_ref, keys_ref, source_ref, far_ref, near_ref, both, sorted_keys, slots, semaphores):
    count, depth = keys_ref.shape
    _, rows, width = slots.shape
    half = count // 2
    height = count // places_ref.shape[0]
    marks = chunk_rows(depth, rows, True)
    slices = [(pl.ds(at, end - at), pl.ds(0, width)) for at, end in marks]

    def use(t, slot):
        if t == 0:
            for i in range(count // height):
                start = pl.multiple_of(places_ref[i] * height, 8)
                sorted_keys[i * height : (i + 1) * height, :] = keys_ref[pl.ds(start, height), :]
            both[:count], both[count:] = split(sorted_keys[...])
        at, end = marks[t]
        found = split_product(both[:, at:end], slot[: end - at, :], PLAIN)
        far_ref[...] = far_ref[...] + found[:half] if t else found[:half]
        near_ref[...] = near_ref[...] + found[half:] if t else found[half:]

    stream(source_ref, slices, slots, semaphores, use)


def fitted_part(keys, weight, places):
    count, depth = keys.shape
    width = weight.shape[1]
    rows = tile_of(depth, WEIGHT_ROWS)
    return pl.pallas_call(
        fitted_kernel,
        out_shape=[floats(count // 2, width)] * 2,
        in_specs=[
            pl.BlockSpec(memory_space=pltpu.SMEM),
            pl.BlockSpec(memory_space=pltpu.VMEM),
            pl.BlockSpec(memory_space=pl.ANY),
        ],
        scratch_shapes=[
            pltpu.VMEM((2 * count, depth), jnp.bfloat16),
            pltpu.VMEM((count, depth), jnp.float32),
            pltpu.VMEM((WEIGHT_SLOTS, rows, width), jnp.float32),
            pltpu.SemaphoreType.DMA((WEIGHT_SLOTS,)),
        ],
        **settings(6 * count * depth * width, 4 * depth * width),
    )(places, keys, weight)


def moments_kernel(col_ref, keys_ref, piece_ref, share_ref, out_ref):
    width = share_ref.shape[1]
    for i in range(keys_ref.shape[1] // width):

        @pl.when(col_ref[0] == i)
        def _():
            part = keys_ref[:, i * width : (i + 1) * width]
            out_ref[0] = precise(part, share_ref[...], ACROSS)

    out_ref[1] = precise(piece_ref[...], piece_ref[...], ACROSS)
    out_ref[2] = precise(keys_ref[...], keys_ref[...], ACROSS)


def moments(keys, piece, share, col):
    count = keys.shape[0]
    return pl.pallas_call(
        moments_kernel,
        out_shape=floats(3, count, count),
        in_specs=[pl.BlockSpec(memory_space=pltpu.SMEM)]
        + [pl.BlockSpec(memory_space=pltpu.VMEM)] * 3,
        out_specs=pl.BlockSpec(memory_space=pltpu.VMEM),
        **settings(12 * count * count * keys.shape[1], 8 * keys.size),
    )(col.reshape(1), keys, piece, share)


def third_kernel(order_ref, image_ref, *refs):
    *shares, out_ref = refs
    total = jnp.zeros(out_ref.shape, jnp.float32)
    for i, share in enumerate(shares):
        rows = share.shape[1]
        part = image_ref[pl.ds(pl.multiple_of(order_ref[i] * rows, 8), rows), :]
        total = total + precise(share[...], part)
    out_ref[...] = total


def third_moment(shares, image, order):
    count = image.shape[1]
    return pl.pallas_call(
        third_kernel,
        out_shape=floats(count, count),
        in_specs=[pl.BlockSpec(memory_space=pltpu.SMEM)]
        + [pl.BlockSpec(memory_space=pltpu.VMEM)] * (1 + len(shares)),
        **settings(12 * count * image.size, 8 * image.size),
    )(order, image, *shares)


def invert_block(entries, size):
    def entry(i, j):
        return entries[min(i, j), max(i, j)]

    for k in range(size):
        inverse = 1.0 / entry(k, k)
        scaled = [entry(i, k) * inverse for i in range(size)]
        updated = {}
        for i in range(size):
            for j in range(i, size):
                if i != k and j != k:
                    updated[i, j] = entries[i, j] - entry(i, k) * scaled[j]
                elif i == j:
                    updated[i, j] = -inverse
                else:
                    updated[i, j] = scaled[j if i == k else i]
        entries = updated
    return {key: -value for key, value in entries.items()}


def eliminate(work, count, block=8):
    row = lax.broadcasted_iota(jnp.int32, (count, count), 0)
    lane = lax.broadcasted_iota(jnp.int32, (count, count), 1)
    matrix = work[:, :count]
    diagonal = jnp.where(row == lane, matrix, 0.0)
    across = lax.rsqrt(jnp.sum(diagonal, axis=0, keepdims=True))
    down = lax.rsqrt(jnp.sum(diagonal, axis=1, keepdims=True))
    work[:, :count] = matrix * down * across
    work[:, count:] = work[:, count:] * down
    width = work.shape[1]
    for at in range(0, count, block):
        panel = work[at : at + block, :]
        entries = {
            (i, j): jnp.broadcast_to(panel[i : i + 1, at + j : at + j + 1], (1, LANES))
            for i in range(block)
            for j in range(i, block)
        }
        entries = invert_block(entries, block)
        solved = 0.0
        for j in range(block):
            column = jnp.concatenate(
                [entries[min(i, j), max(i, j)] for i in range(block)], axis=0
            )
            column = jnp.concatenate([column] * (width // LANES), axis=1)
            solved = solved + column * panel[j : j + 1, :]
        columns = work[:, at : at + block]
        updated = work[...]
        for j in range(block):
            updated = updated - columns[:, j : j + 1] * solved[j : j + 1, :]
        work[...] = updated
        work[at : at + block, :] = solved
    return work[:, count:] * down


def early_kernel(gram_ref, moments_ref, alpha_ref, basis_ref, right_ref, known_ref, work):
    count = gram_ref.shape[0]
    gram, first, second = gram_ref[...], moments_ref[0], moments_ref[1]
    first = 0.5 * (first + first.T)
    curvature = first + precise(gram, gram)
    curvature = 0.5 * (curvature + curvature.T)
    three = precise(gram, jnp.concatenate([first, second, curvature], axis=1))
    gram_first, gram_second, gram_curvature = (
        three[:, i * count : (i + 1) * count] for i in range(3)
    )
    square = second + gram_first.T + gram_curvature
    work[:, :count], work[:, count : 2 * count], work[:, 2 * count :] = curvature, square, gram
    solved = eliminate(work, count)
    two = precise(square, solved)
    alpha_ref[...] = solved[:, count:]
    basis_ref[...] = gram - solved[:, :count]
    right_ref[...] = curvature - two[:, count:]
    known_ref[...] = (
        gram_second
        + gram_second.T
        + precise(gram_first, gram)
        + precise(curvature, curvature)
        - two[:, :count]
    )


def early_solve(gram, pair):
    count = gram.shape[0]
    return pl.pallas_call(
        early_kernel,
        out_shape=[floats(count, count)] * 4,
        scratch_shapes=[pltpu.VMEM((count, 3 * count), jnp.float32)],
        **settings(60 * count**3, 32 * count**2),
    )(gram, pair)


def upright_kernel(order_ref, keys_ref, *refs):
    *shares, high_ref, low_ref = refs
    count = keys_ref.shape[0]
    high_ref[:, :count], low_ref[:, :count] = split(keys_ref[...].T)
    for i, share in enumerate(shares):
        rows = share.shape[1]
        part = pl.ds(pl.multiple_of(order_ref[i] * rows, 16), rows)
        high_ref[part, count:], low_ref[part, count:] = split(share[...].T)


def upright(keys, shares, order):
    count, depth = keys.shape
    tall = jax.ShapeDtypeStruct((depth, 2 * count), jnp.bfloat16)
    return pl.pallas_call(
        upright_kernel,
        out_shape=[tall, tall],
        in_specs=[pl.BlockSpec(memory_space=pltpu.SMEM)]
        + [pl.BlockSpec(memory_space=pltpu.VMEM)] * (1 + len(shares)),
        **settings(count * depth, 16 * count * depth),
    )(order, keys, *shares)


def increment_kernel(
    places_ref, third_ref, known_ref, right_ref, alpha_ref, basis_ref, targets_ref, fitted_ref,
    high_ref, low_ref,
    out_ref, right_high, right_low, work, residual,
):
    count = third_ref.shape[0]

    @pl.when(pl.program_id(0) == 0)
    def _():
        matrix = third_ref[...] + known_ref[...]
        work[:, :count], work[:, count:] = 0.5 * (matrix + matrix.T), right_ref[...]
        gamma = eliminate(work, count)
        height = count // places_ref.shape[0]
        for i in range(count // height):
            part = pl.ds(pl.multiple_of(places_ref[i] * height, 8), height)
            residual[part, :] = targets_ref[part, :] - fitted_ref[i * height : (i + 1) * height, :]
        lower = triple(gamma, residual[...])
        upper = triple(alpha_ref[...], residual[...]) + triple(basis_ref[...], lower)
        right_high[:count], right_low[:count] = split(upper)
        right_high[count:], right_low[count:] = split(lower)

    out_ref[...] = (
        jnp.dot(high_ref[...], right_high[...], preferred_element_type=jnp.float32)
        + jnp.dot(low_ref[...], right_high[...], preferred_element_type=jnp.float32)
        + jnp.dot(high_ref[...], right_low[...], preferred_element_type=jnp.float32)
    )


def increment_product(third, known, right, alpha, basis, targets, fitted, high, low, places):
    rows, depth = high.shape
    width = targets.shape[1]
    tile = tile_of(rows, 512)
    left = pl.BlockSpec((tile, depth), lambda j: (j, 0))
    square = pl.BlockSpec(third.shape, lambda j: (0, 0))
    return pl.pallas_call(
        increment_kernel,
        out_shape=floats(rows, width),
        grid=(rows // tile,),
        in_specs=[pl.BlockSpec(memory_space=pltpu.SMEM)]
        + [square] * 5
        + [pl.BlockSpec(targets.shape, lambda j: (0, 0))] * 2 + [left] * 2,
        out_specs=pl.BlockSpec((tile, width), lambda j: (j, 0)),
        scratch_shapes=[pltpu.VMEM((depth, width), jnp.bfloat16)] * 2
        + [pltpu.VMEM((third.shape[0], depth), jnp.float32), pltpu.VMEM(targets.shape, jnp.float32)],
        **settings(6 * depth * rows * width, 4 * (depth * rows + depth * width + rows * width)),
    )(places, third, known, right, alpha, basis, targets, fitted, high, low)


def swap(value, mask):
    return lax.ppermute(value, "row", [(i, i ^ mask) for i in range(lax.axis_size("row"))])


def others(value):
    count = lax.axis_size("col")
    return [
        lax.ppermute(value, "col", [(i, (i + d) % count) for i in range(count)])
        for d in range(1, count)
    ]


def chip_masks():
    return range(2, lax.axis_size("row"), 2)


def sum_over_row(value):
    value = value + swap(value, 1)
    return sum((swap(value, mask) for mask in chip_masks()), value)


def sum_over_col(value):
    return sum(others(value), value)


def row_masks():
    masks, order = [], [0]
    mask = 1
    while mask < lax.axis_size("row"):
        masks.append(mask)
        mask *= 2
    for mask in reversed(masks):
        order = order + [i | mask for i in order]
    return masks, order


def after(value, *earlier):
    return lax.optimization_barrier((value, *earlier))[0]


def to_rows(value, k):
    rows, cols = lax.axis_size("row"), lax.axis_size("col")
    blocks, chips = rows // cols, rows // 2
    pairs = []
    for row in range(rows):
        place = (row % 2) * chips + row // 2
        for col in range(cols):
            target = (blocks * col + place // cols) * cols + (place % cols - k) % cols
            pairs.append((row * cols + col, target))
    return lax.ppermute(value, ("row", "col"), pairs)


def body(key_rows, targets, weight, covariance):
    rows, cols = lax.axis_size("row"), lax.axis_size("col")
    row, col = lax.axis_index("row"), lax.axis_index("col")
    chips, core, chip = rows // 2, row % 2, row // 2
    count = key_rows.shape[0] * cols
    width = covariance.shape[1] // rows
    near = jnp.bitwise_xor(jnp.arange(chips, dtype=jnp.int32), chip)
    mine, theirs = core * chips + near, (1 - core) * chips + near
    places = jnp.concatenate([theirs, mine])
    masks, levels = row_masks()
    ranks = jnp.bitwise_xor(jnp.array(levels, dtype=jnp.int32), row)
    order = (col + jnp.arange(cols, dtype=jnp.int32)) % cols

    parts = 2 if key_rows.shape[1] % (2 * LANES) == 0 else 1
    depth = key_rows.shape[1] // parts
    sent, received = None, []
    for part in range(parts):
        block = key_rows[:, part * depth : (part + 1) * depth]
        received.append([block, *others(block if sent is None else after(block, *sent))])
        sent = received[-1][1:]
    key_parts, pieces = [], None
    for part in range(parts):
        keys = jnp.zeros((cols, key_rows.shape[0], depth), key_rows.dtype)
        for d, block in enumerate(received[part]):
            keys = lax.dynamic_update_index_in_dim(keys, block, (col - d) % cols, 0)
        key_parts.append(keys.reshape(count, -1))
        if part < parts - 1:
            pieces = image_pieces(key_parts[part], covariance, places, width, part, pieces)
    last = key_parts[-1]
    far_part = image_pieces(last, covariance, theirs, width, parts - 1, pieces)
    last = after(last, far_part)
    near_part = image_pieces(last, covariance, mine, width, parts - 1, pieces, chips)
    part = near_part + swap(far_part, 1)
    piece = sum((swap(part[mask // 2], mask) for mask in chip_masks()), part[0])

    keys = jnp.concatenate([after(block, part) for block in key_parts], axis=1)
    half = rows // 2
    fitted_far, fitted = fitted_part(keys, weight, jnp.concatenate([ranks[half:], ranks[:half]]))
    piece, fitted_far, fitted = lax.optimization_barrier((piece, fitted_far, fitted))
    near_pieces = jnp.stack([piece, *[swap(piece, mask) for mask in chip_masks()]])
    fitted = fitted + swap(fitted_far, 1)

    def halve(value, mask):
        keep = value.shape[0] // 2
        return value[:keep] + swap(value[keep:], mask)

    def double(value, mask):
        return jnp.concatenate([value, swap(value, mask)], axis=0)

    chain = [(halve, mask) for mask in masks[1:]] + [(double, mask) for mask in reversed(masks)]

    def advance(value, steps):
        for _ in range(steps):
            if chain:
                move, mask = chain.pop(0)
                value = move(value, mask)
        return value

    far_pieces = swap(near_pieces, 1)
    held = after(piece, near_pieces)
    shares = [to_rows(held, k) for k in range(cols - 1)]

    applied = apply_pieces(near_pieces, covariance, mine)
    sums = moments(keys, after(piece, applied), shares[0], col)
    far_pieces, applied, sums, *shares = lax.optimization_barrier(
        (far_pieces, applied, sums, *shares)
    )
    middle = max(chips // 2, 2)
    shares.append(to_rows(after(piece, *shares), cols - 1))
    sums = sums + swap(sums, 1)
    fitted = advance(fitted, 1)
    applied = apply_pieces(far_pieces, covariance, theirs, applied, 0, middle)
    applied, sums, fitted = lax.optimization_barrier((applied, sums, fitted))
    sums = sum((swap(sums, mask) for mask in chip_masks()), sums)
    fitted = advance(fitted, 1)
    if middle < chips:
        applied = apply_pieces(far_pieces, covariance, theirs, applied, middle, chips - middle)
    applied, sums, fitted = lax.optimization_barrier((applied, sums, fitted))
    gram = sums[2]

    pair = sum_over_col(sums[:2])
    third = third_moment(shares, applied, order)
    tall = upright(after(keys, third), shares, order)
    third = third + swap(third, 1)
    fitted = advance(fitted, 1)
    third, fitted, gram, *tall = lax.optimization_barrier((third, fitted, gram, *tall))
    third = sum((swap(third, mask) for mask in chip_masks()), third)
    fitted = advance(fitted, 1)
    early = early_solve(gram, pair)
    third, fitted, *early = lax.optimization_barrier((third, fitted, *early))
    third = sum_over_col(third)
    fitted = advance(fitted, len(chain))
    alpha, basis, right, known = early
    tall_high, tall_low = tall
    return increment_product(
        third, known, right, alpha, basis, targets, fitted, tall_high, tall_low, ranks
    )


def solution(mesh):
    placed = (P("col", "row"), P(None, "col"), P("row", "col"), P("row", "col"))
    return jax.shard_map(
        body, mesh=mesh, in_specs=placed, out_specs=P("row", "col"), check_vma=False
    )
```
